32 devices in a mesh: gx: 4 (over z), gy: 8 (over y, x, core).
Axes of the slice: x: 2, y: 2, z: 4, core: 2. Of those that a mesh axis runs over, the one named last changes fastest.
Arguments:
- orbitals: bfloat16 [24, 48, 11, 256], P('gx', 'gy'), may hold values from -140 to 140, as said below
- masses: float32 [24, 48, 11], P('gx', 'gy'), may hold values from 0.5 to 2, as said below
- cell_matrices: bfloat16 [4, 8, 2, 216, 216], P('gx', 'gy'), may hold values from -0.12 to 3.12, as said below
Outputs:
- filtered_orbitals: bfloat16 [24, 48, 11, 256], P('gx', 'gy')
The draws below stay inside these ranges and needn't reach their ends.
Inputs may be any that keep to these rules, and one draw needn't show every extreme that they name: Entries of orbitals that hold the same mesh node are equal. Entries of masses that hold the same mesh node are equal. `cell_matrices`: every cell matrix is symmetric.
All inputs are finite; a program needn't handle non-finite values.
Results may differ from the reference program's by a relative error of at most 0.0063.
The reference program's roundings to bfloat16 on the way count: a program that leaves them out, or rounds other values in their place, can miss the bound.
Values sent between devices are 32-bit elements; how exact they have to be, the bound alone decides.
A program may use at most 64 MiB of HBM per device.

```python
import math
import jax
import jax.numpy as jnp
from jax import lax

ORBS = 256
CX = 1
CY = 1
CZ = 2
FILTER_DEG = 3
NS_STEPS = 2
N_GX = 4
N_GY = 8


def repeat_rims_drawn(array, along_dim, device_count, cells_along):
    layers = 5 * cells_along
    positions = jnp.arange(device_count * (layers + 1), dtype=jnp.int32)
    source = (positions // (layers + 1) * layers + positions % (layers + 1)) % (device_count * layers)
    return jnp.take(array, source.astype(jnp.int32), axis=along_dim)


def draw_orbitals(key, part):
    nodes_x = 5 * CX * N_GX
    nodes_y = 5 * CY * N_GY
    depth = 5 * CZ + 1
    shape = (nodes_x, nodes_y, depth, ORBS)
    value_key = jax.random.fold_in(key, 11)
    pair_key = jax.random.fold_in(key, 12)
    values = jnp.clip(jax.random.normal(value_key, shape, jnp.float32), -4.0, 4.0)
    pairing = jax.random.permutation(pair_key, N_GY)
    column_block = jnp.arange(nodes_y, dtype=jnp.int32) // (5 * CY)
    orbital_group = jnp.arange(ORBS, dtype=jnp.int32) % N_GY
    spiked = pairing[column_block][:, None] == orbital_group[None, :]
    values = values * jnp.where(spiked, 8.0, 1.0)[None, :, None, :]
    values = repeat_rims_drawn(values, 0, N_GX, CX)
    values = repeat_rims_drawn(values, 1, N_GY, CY)
    return values.astype(jnp.bfloat16)


def draw_masses(key, part):
    nodes_x = 5 * CX * N_GX
    nodes_y = 5 * CY * N_GY
    depth = 5 * CZ + 1
    shape = (nodes_x, nodes_y, depth)
    mass_key = jax.random.fold_in(key, 21)
    values = jnp.exp(jax.random.uniform(mass_key, shape, jnp.float32, math.log(0.5), math.log(2.0)))
    values = repeat_rims_drawn(values, 0, N_GX, CX)
    values = repeat_rims_drawn(values, 1, N_GY, CY)
    return values.astype(jnp.float32)


def draw_cell_matrices(key, part):
    shape = (CX * N_GX, CY * N_GY, CZ, 216, 216)
    noise_key = jax.random.fold_in(key, 31)
    diag_key = jax.random.fold_in(key, 32)
    noise = 0.03 * jnp.clip(jax.random.normal(noise_key, shape, jnp.float32), -4.0, 4.0)
    symmetric = 0.5 * (noise + jnp.swapaxes(noise, -1, -2))
    diagonal = jax.random.uniform(diag_key, shape[:-1], jnp.float32, 1.5, 3.0)
    identity = jnp.eye(216, dtype=jnp.float32)
    return (symmetric + identity * diagonal[..., None]).astype(jnp.bfloat16)


def setup_inputs(seed: int = 0) -> dict:
    arg_keys = jax.random.split(jax.random.key(seed), 4)
    return {
        "orbitals": draw_orbitals(jax.random.fold_in(arg_keys[3], 71), 0),
        "masses": draw_masses(jax.random.fold_in(arg_keys[3], 71), 0),
        "cell_matrices": draw_cell_matrices(jax.random.fold_in(arg_keys[3], 71), 0),
    }


center_shift = 12.0
half_span = 12.0

def unfold_cells(values, along_dim, cells_along):
    moved = jnp.moveaxis(values, along_dim, 0)
    trailing = moved.shape[1:]
    main_part = moved[:5 * cells_along].reshape((cells_along, 5) + trailing)
    far_layer = moved[5::5][:, None]
    window = jnp.concatenate([main_part, far_layer], 1)
    return jnp.moveaxis(window, (0, 1), (along_dim, along_dim + 1))

def fold_cells(window, along_dim, cells_along):
    moved = jnp.moveaxis(window, (along_dim, along_dim + 1), (0, 1))
    trailing = moved.shape[2:]
    leading = jnp.concatenate([moved[:, :5], jnp.zeros((1, 5) + trailing, moved.dtype)], 0)
    carried = jnp.concatenate([jnp.zeros((1,) + trailing, moved.dtype), moved[:, 5]], 0)
    leading = leading.at[:, 0].add(carried)
    flattened = leading.reshape((5 * (cells_along + 1),) + trailing)[:5 * cells_along + 1]
    return jnp.moveaxis(flattened, 0, along_dim)

def to_cells(values, cells_x, cells_y, cells_z):
    window = unfold_cells(values, 0, cells_x)
    window = unfold_cells(window, 2, cells_y)
    window = unfold_cells(window, 4, cells_z)
    window = jnp.transpose(window, (0, 2, 4, 1, 3, 5, 6))
    return window.reshape((cells_x, cells_y, cells_z, 216, window.shape[-1]))

def from_cells(products, cells_x, cells_y, cells_z):
    window = products.reshape((cells_x, cells_y, cells_z, 6, 6, 6, products.shape[-1]))
    window = jnp.transpose(window, (0, 3, 1, 4, 2, 5, 6))
    window = fold_cells(window, 4, cells_z)
    window = fold_cells(window, 2, cells_y)
    return fold_cells(window, 0, cells_x)

def inverse_root(intersection):
    frob_norm = jnp.sqrt(jnp.sum(intersection * intersection))
    current = intersection / frob_norm
    identity = jnp.eye(intersection.shape[0], dtype=jnp.float32)
    factor_z = identity
    for sweep_index in range(NS_STEPS):
        step_t = 1.5 * identity - 0.5 * jnp.dot(factor_z, current, precision=lax.Precision.HIGHEST)
        current = jnp.dot(current, step_t, precision=lax.Precision.HIGHEST)
        factor_z = jnp.dot(step_t, factor_z, precision=lax.Precision.HIGHEST)
    return factor_z / jnp.sqrt(frob_norm)

def interior(array, layers_x, layers_y):
    trailing = array.shape[2:]
    first_count = array.shape[0] // layers_x
    second_count = array.shape[1] // layers_y
    blocked = array.reshape((first_count, layers_x, second_count, layers_y) + trailing)
    blocked = blocked[:, :layers_x - 1, :, :layers_y - 1]
    return blocked.reshape((first_count * (layers_x - 1), second_count * (layers_y - 1)) + trailing)

def repeat_rims(array, along_dim, device_count, cells_along):
    layers = 5 * cells_along
    positions = jnp.arange(device_count * (layers + 1), dtype=jnp.int32)
    source = (positions // (layers + 1) * layers + positions % (layers + 1)) % (device_count * layers)
    return jnp.take(array, source.astype(jnp.int32), axis=along_dim)

def reference(orbitals, masses, cell_matrices):
    cells_gx, cells_gy, cells_z = cell_matrices.shape[:3]
    layers_x = 5 * CX + 1
    layers_y = 5 * CY + 1
    nodes_x = 5 * cells_gx
    nodes_y = 5 * cells_gy
    depth = orbitals.shape[2]
    orb_count = orbitals.shape[3]
    node_field = interior(orbitals, layers_x, layers_y)
    node_mass = interior(masses, layers_x, layers_y)
    matrices = cell_matrices.astype(jnp.float32)

    def apply_operator(values):
        extended = jnp.concatenate([values, values[:1]], 0)
        extended = jnp.concatenate([extended, extended[:, :1]], 1)
        cell_vectors = to_cells(extended, cells_gx, cells_gy, cells_z)
        products = jnp.einsum('abcij,abcjo->abcio', matrices, cell_vectors, precision=lax.Precision.HIGHEST)
        assembled = from_cells(products, cells_gx, cells_gy, cells_z)
        assembled = assembled[:nodes_x].at[0].add(assembled[nodes_x])
        assembled = assembled[:, :nodes_y].at[:, 0].add(assembled[:, nodes_y])
        return assembled / node_mass[..., None]
    block_width = math.gcd(orb_count, 32)
    orbital_blocks = jnp.moveaxis(node_field.reshape((nodes_x, nodes_y, depth, orb_count // block_width, block_width)), 3, 0)

    def filter_block(block):
        starting = block.astype(jnp.float32)
        previous = starting
        current = (apply_operator(starting) - center_shift * starting) / half_span
        for sweep_index in range(FILTER_DEG - 1):
            rounded = lax.optimization_barrier(current.astype(jnp.bfloat16)).astype(jnp.float32)
            following = 2.0 * (apply_operator(rounded) - center_shift * current) / half_span - previous
            previous = current
            current = following
        return current
    filtered = lax.map(filter_block, orbital_blocks)
    filtered = jnp.moveaxis(filtered, 0, 3).reshape((nodes_x, nodes_y, depth, orb_count))
    node_rows = filtered.reshape((-1, orb_count))
    weighted = node_rows * node_mass.reshape((-1, 1))
    intersection = jnp.einsum('no,np->op', weighted, node_rows, precision=lax.Precision.HIGHEST) / (nodes_x * nodes_y * depth)
    factor = inverse_root(intersection)
    result = jnp.dot(node_rows, factor, precision=lax.Precision.HIGHEST).astype(jnp.bfloat16)
    result = result.reshape((nodes_x, nodes_y, depth, orb_count))
    result = repeat_rims(result, 0, N_GX, CX)
    result = repeat_rims(result, 1, N_GY, CY)
    return result
```

```python
import functools

import jax
import jax.numpy as jnp
import numpy as np
from jax import lax
from jax.experimental import pallas as pl
from jax.experimental.pallas import tpu as pltpu
from jax.sharding import PartitionSpec as P

FILTER_DEG = 3
CENTER_SHIFT = 12.0
HALF_SPAN = 12.0

RIM = 256
ROWS = 448
INNER = ROWS - RIM
SIDE = 80
CORNER = 16
BF16 = jnp.bfloat16
F32 = jnp.float32

MESSAGES = (
    (-1, 0, 0, SIDE),
    (1, 0, 128, SIDE),
    (0, 1, 64, SIDE),
    (0, -1, 192, SIDE),
    (-1, -1, 0, CORNER),
    (-1, 1, 64, CORNER),
    (1, 1, 128, CORNER),
    (1, -1, 192, CORNER),
)


def column_starts():
    starts = {(0, 0): 0, (0, 5): 64, (5, 5): 128, (5, 0): 192}
    for i in range(4):
        starts[(0, i + 1)] = 16 + 12 * i
        starts[(i + 1, 5)] = 80 + 12 * i
        starts[(5, i + 1)] = 144 + 12 * i
        starts[(i + 1, 0)] = 208 + 12 * i
    for i in range(4):
        for j in range(4):
            starts[(i + 1, j + 1)] = RIM + 12 * (4 * i + j)
    return starts


STARTS = column_starts()


def tables():
    to_rows = np.zeros((2, ROWS, 216), np.float32)
    to_columns = np.zeros((2, 216, ROWS), np.float32)
    pick_xy = np.zeros((ROWS, 48), np.float32)
    pick_z = np.zeros((3, ROWS, 128), np.float32)
    pick_z[2] = 1.0
    for (x, y), start in STARTS.items():
        for half in range(2):
            for k in range(6):
                row = start + 6 * half + k
                z = 5 * half + k
                for cell in range(2):
                    if 0 <= z - 5 * cell <= 5:
                        to_rows[cell, row, (x * 6 + y) * 6 + z - 5 * cell] = 1
                to_columns[half, (x * 6 + y) * 6 + k, row] = 1
                pick_xy[row, 8 * x + y] = 1
                pick_z[0, row, z] = 1
                pick_z[2, row, :] = 0
                if x < 5 and y < 5 and not (half == 1 and k == 0):
                    pick_z[1, row, z] = 1
    return (
        to_rows.astype(BF16),
        to_columns.astype(BF16),
        pick_xy,
        pick_z,
    )


def dot(a, b):
    return jnp.dot(a, b, preferred_element_type=F32)


def dot_rows(a, b):
    return lax.dot_general(a, b, (((0,), (0,)), ((), ())), preferred_element_type=F32)


def split(a):
    high = a.astype(BF16)
    return high, (a - high.astype(F32)).astype(BF16)


def dot3(a, b):
    a_high, a_low = split(a)
    b_high, b_low = split(b)
    return dot(a_high, b_high) + (dot(a_high, b_low) + dot(a_low, b_high))


def gram(rows, weight):
    a_high, a_low = split(rows * weight)
    b_high, b_low = split(rows)

    def part(lanes, columns):
        return dot_rows(a_high[:, lanes], b_high[:, columns]) + (
            dot_rows(a_high[:, lanes], b_low[:, columns])
            + dot_rows(a_low[:, lanes], b_high[:, columns])
        )

    top = part(slice(0, 128), slice(0, 256))
    return top[:, :128], top[:, 128:], part(slice(128, 256), slice(128, 256))


def inverse_root(stacked, node_total):
    s00, s01, s11 = stacked[0:128], stacked[128:256], stacked[256:384]
    top = jnp.concatenate([s00, s01], axis=1)
    bottom = jnp.concatenate([s01.T, s11], axis=1)
    inter = jnp.concatenate([top, bottom], axis=0) * (1.0 / node_total)
    frob2 = jnp.sum(jnp.sum(inter * inter, axis=1, keepdims=True), axis=0, keepdims=True)
    frob = jnp.sqrt(frob2)
    current = inter / frob
    row_id = lax.broadcasted_iota(jnp.int32, (256, 256), 0)
    col_id = lax.broadcasted_iota(jnp.int32, (256, 256), 1)
    identity = jnp.where(row_id == col_id, 1.0, 0.0).astype(F32)
    square = dot3(current, current)
    tail = 1.6875 * identity - 0.5625 * current + 0.0625 * square
    factor_z = 2.25 * identity - 2.4375 * current + dot3(square, tail)
    return factor_z / jnp.sqrt(frob)


def filter_phase(sizes, orbitals, masses, cells, to_rows, to_columns, pick_xy, pick_z,
                 matrix, mass_pad, states, rounded, sent, arrived, send_sems, recv_sems,
                 before_first_send):
    n_gx, n_gy = sizes
    my_x, my_y = lax.axis_index("gx"), lax.axis_index("gy")

    states[0] = jnp.zeros((ROWS, 256), F32)
    for (x, y), start in STARTS.items():
        column = orbitals[x, y].astype(F32)
        states[0, start : start + 6] = column[0:6]
        states[0, start + 6 : start + 12] = column[5:11]
    rounded[...] = states[0].astype(BF16)

    first = dot(to_rows[0], cells[0, 0, 0]).astype(BF16)
    second = dot(to_rows[1], cells[0, 0, 1]).astype(BF16)
    matrix[...] = (dot(first, to_columns[0]) + dot(second, to_columns[1])).astype(BF16)

    mass_pad[...] = jnp.zeros(mass_pad.shape, F32)
    for x in range(6):
        mass_pad[8 * x : 8 * x + 6, 0:11] = masses[x]
    spread = jnp.dot(
        pick_xy[...], mass_pad[...], preferred_element_type=F32, precision=lax.Precision.HIGHEST
    )
    mass = jnp.sum(spread * pick_z[0], axis=1, keepdims=True) + pick_z[2, :, 0:1]
    weight = jnp.sum(spread * pick_z[1], axis=1, keepdims=True)
    scale1 = 1.0 / (HALF_SPAN * mass)
    shift = CENTER_SHIFT / HALF_SPAN

    def copies(step):
        out = []
        for index, (dx, dy, first_row, rows) in enumerate(MESSAGES):
            target = (lax.rem(my_x + dx + n_gx, n_gx), lax.rem(my_y + dy + n_gy, n_gy))
            landing = arrived.at[step, pl.ds(80 * index, rows)] if rows == SIDE else arrived.at[
                step, pl.ds(320 + 16 * (index - 4), rows)
            ]
            out.append(
                pltpu.make_async_remote_copy(
                    src_ref=sent.at[step, pl.ds(first_row, rows)],
                    dst_ref=landing,
                    send_sem=send_sems.at[step, index],
                    recv_sem=recv_sems.at[step, index],
                    device_id=target,
                    device_id_type=pl.DeviceIdType.MESH,
                )
            )
        return out

    def received(step, index, low, high):
        base = 80 * index if index < 4 else 320 + 16 * (index - 4)
        return arrived[step, base + low : base + high]

    def advance(step, product, rows):
        if step == 0:
            return product * scale1[rows] - shift * states[0, rows]
        return (2.0 * product) * scale1[rows] - (2.0 * shift) * states[step, rows] - states[step - 1, rows]

    rim, inner = slice(0, RIM), slice(RIM, ROWS)
    ahead = dot(matrix[rim, inner], rounded[inner])
    grams = None
    everything = []
    for step in range(FILTER_DEG):
        product = ahead + dot(matrix[rim, rim], rounded[rim])
        sent[step, 0:RIM] = product
        sent[step, RIM : RIM + CORNER] = product[0:CORNER]
        if step == 0:
            before_first_send()
        moves = copies(step)
        everything += moves
        for move in moves:
            move.start()
        last = step == FILTER_DEG - 1
        inner_next = advance(step, dot(matrix[inner], rounded[...]), inner)
        states[step + 1, inner] = inner_next
        if last:
            grams = gram(inner_next, weight[inner])
        else:
            rounded[inner] = inner_next.astype(BF16)
            ahead = dot(matrix[rim, inner], rounded[inner])
        for move in moves:
            move.wait_recv()
        own = lambda low, high: sent[step, low:high]
        got = functools.partial(received, step)
        summed = jnp.concatenate(
            [
                own(0, 16) + got(1, 64, 80) + got(2, 0, 16) + got(6, 0, 16),
                own(16, 64) + got(1, 16, 64),
                own(64, 80) + got(1, 0, 16) + got(3, 64, 80) + got(7, 0, 16),
                own(80, 128) + got(3, 16, 64),
                own(128, 144) + got(0, 64, 80) + got(3, 0, 16) + got(4, 0, 16),
                own(144, 192) + got(0, 16, 64),
                own(192, 208) + got(0, 0, 16) + got(2, 64, 80) + got(5, 0, 16),
                own(208, 256) + got(2, 16, 64),
            ],
            axis=0,
        )
        rim_next = advance(step, summed, rim)
        states[step + 1, rim] = rim_next
        if last:
            owned = jnp.concatenate([rim_next[0:64], rim_next[208:256]], axis=0)
            owned_weight = jnp.concatenate([weight[0:64], weight[208:256]], axis=0)
            grams = tuple(a + b for a, b in zip(grams, gram(owned, owned_weight)))
        else:
            rounded[rim] = rim_next.astype(BF16)
    return grams, everything


def rotate_phase(filtered, factor, out):
    result = dot3(filtered, factor)
    for (x, y), start in STARTS.items():
        column = jnp.concatenate(
            [result[start : start + 6], result[start + 7 : start + 12]], axis=0
        )
        out[x, y] = column.astype(BF16)


def greet(peers):
    barrier = pltpu.get_barrier_semaphore()
    for peer in peers:
        pl.semaphore_signal(barrier, inc=1, device_id=peer, device_id_type=pl.DeviceIdType.MESH)
    return lambda: pl.semaphore_wait(barrier, len(peers))


def halo_offsets():
    return [(dx, dy) for dx, dy, _, _ in MESSAGES]


def at_offset(sizes, offset):
    n_gx, n_gy = sizes
    return (
        lax.rem(lax.axis_index("gx") + (offset[0] + n_gx), n_gx),
        lax.rem(lax.axis_index("gy") + (offset[1] + n_gy), n_gy),
    )


def fused_kernel(sizes, node_total, orbitals, masses, cells, to_rows, to_columns, pick_xy, pick_z,
                 out, matrix, mass_pad, states, rounded, sent, arrived, send_sems, recv_sems,
                 own, row_in, part, column_in, whole,
                 row_send, row_recv, col_send, col_recv, all_send, all_recv):
    n_gx, n_gy = sizes
    my_y = lax.axis_index("gy")
    offsets = {(dx % n_gx, dy % n_gy) for dx, dy in halo_offsets()}
    offsets |= {(0, d) for d in range(1, n_gy)} | {(d, 0) for d in range(1, n_gx)}
    wait_all = greet([at_offset(sizes, offset) for offset in sorted(offsets)])
    grams, moves = filter_phase(
        sizes, orbitals, masses, cells, to_rows, to_columns, pick_xy, pick_z,
        matrix, mass_pad, states, rounded, sent, arrived, send_sems, recv_sems, wait_all,
    )
    chunk = own.shape[1]
    per_block = 128 // chunk if 128 % chunk == 0 else None
    stacked = jnp.concatenate(grams, axis=0)
    for index in range(n_gy):
        own[index] = stacked[index * chunk : (index + 1) * chunk]

    def remote(src, dst, send, recv, offset):
        return pltpu.make_async_remote_copy(
            src_ref=src, dst_ref=dst, send_sem=send, recv_sem=recv,
            device_id=at_offset(sizes, offset), device_id_type=pl.DeviceIdType.MESH,
        )

    row_moves = [
        remote(own.at[lax.rem(my_y + d, n_gy)], row_in.at[d - 1], row_send.at[d - 1],
               row_recv.at[d - 1], (0, d))
        for d in range(1, n_gy)
    ]
    for move in row_moves:
        move.start()
    for move in row_moves:
        move.wait_recv()
    total = own[my_y]
    for d in range(1, n_gy):
        total = total + row_in[d - 1]
    part[...] = total
    col_moves = [
        remote(part, column_in.at[d - 1], col_send.at[d - 1], col_recv.at[d - 1], (d, 0))
        for d in range(1, n_gx)
    ]
    for move in col_moves:
        move.start()
    for move in col_moves:
        move.wait_recv()
    for d in range(1, n_gx):
        total = total + column_in[d - 1]
    whole[my_y] = total
    all_moves = [
        remote(whole.at[my_y], whole.at[my_y], all_send.at[d - 1], all_recv.at[d - 1], (0, d))
        for d in range(1, n_gy)
    ]
    for move in all_moves:
        move.start()
    for move in all_moves:
        move.wait_recv()
    stacked = jnp.concatenate([whole[index] for index in range(n_gy)], axis=0)
    factor = inverse_root(stacked, node_total)
    rotate_phase(states[FILTER_DEG], factor, out)
    for move in moves + row_moves + col_moves + all_moves:
        move.wait_send()


def filter_kernel(sizes, orbitals, masses, cells, to_rows, to_columns, pick_xy, pick_z,
                  filtered, stacked, matrix, mass_pad, states, rounded, sent, arrived,
                  send_sems, recv_sems):
    wait_all = greet([at_offset(sizes, offset) for offset in halo_offsets()])
    grams, moves = filter_phase(
        sizes, orbitals, masses, cells, to_rows, to_columns, pick_xy, pick_z,
        matrix, mass_pad, states, rounded, sent, arrived, send_sems, recv_sems, wait_all,
    )
    stacked[...] = jnp.concatenate(grams, axis=0)
    filtered[...] = states[FILTER_DEG]
    for move in moves:
        move.wait_send()


def rotate_kernel(node_total, filtered, stacked, out):
    rotate_phase(filtered[...], inverse_root(stacked[...], node_total), out)


def body(orbitals, masses, cell_matrices):
    n_gx, n_gy = lax.axis_size("gx"), lax.axis_size("gy")
    sizes = (n_gx, n_gy)
    assert orbitals.shape == (6, 6, 11, 256) and cell_matrices.shape == (1, 1, 2, 216, 216)
    node_total = 5 * n_gx * 5 * n_gy * 11
    constants = tuple(jnp.asarray(t) for t in tables())
    vmem = pl.BlockSpec(memory_space=pltpu.VMEM)
    count = len(MESSAGES)
    filter_scratch = [
        pltpu.VMEM((ROWS, ROWS), BF16),
        pltpu.VMEM((48, 128), F32),
        pltpu.VMEM((FILTER_DEG + 1, ROWS, 256), F32),
        pltpu.VMEM((ROWS, 256), BF16),
        pltpu.VMEM((FILTER_DEG, RIM + CORNER, 256), F32),
        pltpu.VMEM((FILTER_DEG, 384, 256), F32),
        pltpu.SemaphoreType.DMA((FILTER_DEG, count)),
        pltpu.SemaphoreType.DMA((FILTER_DEG, count)),
    ]
    params = pltpu.CompilerParams(
        collective_id=0, has_side_effects=True, vmem_limit_bytes=48 << 20
    )
    if 384 % (8 * n_gy) == 0:
        chunk = 384 // n_gy
        return pl.pallas_call(
            functools.partial(fused_kernel, sizes, node_total),
            out_shape=jax.ShapeDtypeStruct(orbitals.shape, BF16),
            in_specs=[vmem] * 7,
            out_specs=vmem,
            scratch_shapes=filter_scratch
            + [
                pltpu.VMEM((n_gy, chunk, 128), F32),
                pltpu.VMEM((n_gy - 1, chunk, 128), F32),
                pltpu.VMEM((chunk, 128), F32),
                pltpu.VMEM((n_gx - 1, chunk, 128), F32),
                pltpu.VMEM((n_gy, chunk, 128), F32),
                pltpu.SemaphoreType.DMA((n_gy - 1,)),
                pltpu.SemaphoreType.DMA((n_gy - 1,)),
                pltpu.SemaphoreType.DMA((n_gx - 1,)),
                pltpu.SemaphoreType.DMA((n_gx - 1,)),
                pltpu.SemaphoreType.DMA((n_gy - 1,)),
                pltpu.SemaphoreType.DMA((n_gy - 1,)),
            ],
            compiler_params=params,
        )(orbitals, masses, cell_matrices, *constants)
    filtered, stacked = pl.pallas_call(
        functools.partial(filter_kernel, sizes),
        out_shape=[
            jax.ShapeDtypeStruct((ROWS, 256), F32),
            jax.ShapeDtypeStruct((384, 128), F32),
        ],
        in_specs=[vmem] * 7,
        out_specs=[vmem] * 2,
        scratch_shapes=filter_scratch,
        compiler_params=params,
    )(orbitals, masses, cell_matrices, *constants)
    stacked = lax.psum(stacked, ("gx", "gy"))
    return pl.pallas_call(
        functools.partial(rotate_kernel, node_total),
        out_shape=jax.ShapeDtypeStruct(orbitals.shape, BF16),
        in_specs=[vmem] * 2,
        out_specs=vmem,
        compiler_params=pltpu.CompilerParams(vmem_limit_bytes=48 << 20),
    )(filtered, stacked)


def solution(mesh):
    return jax.shard_map(
        body,
        mesh=mesh,
        in_specs=(P("gx", "gy", None, None), P("gx", "gy", None), P("gx", "gy", None, None, None)),
        out_specs=P("gx", "gy", None, None),
        check_vma=False,
    )
```

```python
import functools

import jax
import jax.numpy as jnp
import numpy as np
from jax import lax
from jax.experimental import pallas as pl
from jax.experimental.pallas import tpu as pltpu
from jax.sharding import PartitionSpec as P

FILTER_DEG = 3
CENTER_SHIFT = 12.0
HALF_SPAN = 12.0

RIM = 240
ROWS = 432
INNER = ROWS - RIM
CORNERS = 48
PIECES = 1
VMEM_BYTES = (64 << 20) - (128 << 10)
BF16 = jnp.bfloat16
F32 = jnp.float32

MESSAGES = (
    (-1, -1, "corner", 0, 3),
    (1, -1, "corner", 1, 2),
    (-1, 1, "corner", 2, 1),
    (1, 1, "corner", 3, 0),
    (-1, 0, "x", 0, 1),
    (1, 0, "x", 1, 0),
    (0, -1, "y", 0, 1),
    (0, 1, "y", 1, 0),
)


def column_starts():
    starts = {(0, 0): 0, (5, 0): 12, (0, 5): 24, (5, 5): 36}
    for i in range(4):
        starts[(0, i + 1)] = 48 + 12 * i
        starts[(5, i + 1)] = 96 + 12 * i
        starts[(i + 1, 0)] = 144 + 12 * i
        starts[(i + 1, 5)] = 192 + 12 * i
    for i in range(4):
        for j in range(4):
            starts[(i + 1, j + 1)] = RIM + 12 * (4 * i + j)
    return starts


STARTS = column_starts()


def tables():
    down = np.zeros((ROWS, 128), np.int32)
    along = np.full((8, ROWS), -1, np.int32)
    for (x, y), start in STARTS.items():
        for half in range(2):
            for k in range(6):
                row, z = start + 6 * half + k, 5 * half + k
                for cell in range(2):
                    inside = 0 <= z - 5 * cell <= 5
                    down[row, cell] = (x * 6 + y) * 6 + z - 5 * cell if inside else -1
                down[row, 2], down[row, 3] = 8 * x + y, z
                down[row, 4] = int(x < 5 and y < 5 and not (half == 1 and k == 0))
                along[half, row] = (x * 6 + y) * 6 + k
    return down, along


def dot(a, b):
    return jnp.dot(a, b, preferred_element_type=F32)


def dot_rows(a, b):
    return lax.dot_general(a, b, (((0,), (0,)), ((), ())), preferred_element_type=F32)


def split(a):
    high = a.astype(BF16)
    return high, (a - high.astype(F32)).astype(BF16)


def dot3(a, b):
    a_high, a_low = split(a)
    b_high, b_low = split(b)
    return dot(a_high, b_high) + (dot(a_high, b_low) + dot(a_low, b_high))


def one_hot(condition):
    return jnp.where(condition, 1.0, 0.0).astype(F32)


def gram(rows, weight):
    a_high, a_low = split(rows * weight)
    b_high, b_low = split(rows)

    def part(lanes, columns):
        return dot_rows(a_high[:, lanes], b_high[:, columns]) + (
            dot_rows(a_high[:, lanes], b_low[:, columns])
            + dot_rows(a_low[:, lanes], b_high[:, columns])
        )

    top = part(slice(0, 128), slice(0, 256))
    return top[:, :128], top[:, 128:], part(slice(128, 256), slice(128, 256))


def inverse_root(stacked, node_total):
    s00, s01, s11 = stacked[0:128], stacked[128:256], stacked[256:384]
    top = jnp.concatenate([s00, s01], axis=1)
    bottom = jnp.concatenate([s01.T, s11], axis=1)
    inter = jnp.concatenate([top, bottom], axis=0) * (1.0 / node_total)
    frob2 = jnp.sum(jnp.sum(inter * inter, axis=1, keepdims=True), axis=0, keepdims=True)
    frob = jnp.sqrt(frob2)
    current = inter / frob
    row_id = lax.broadcasted_iota(jnp.int32, (256, 256), 0)
    col_id = lax.broadcasted_iota(jnp.int32, (256, 256), 1)
    identity = one_hot(row_id == col_id)
    square = dot3(current, current)
    tail = 1.6875 * identity - 0.5625 * current + 0.0625 * square
    factor_z = 2.25 * identity - 2.4375 * current + dot3(square, tail)
    return factor_z / jnp.sqrt(frob)


def at_offset(sizes, offset):
    n_gx, n_gy = sizes
    return (
        lax.rem(lax.axis_index("gx") + (offset[0] + n_gx), n_gx),
        lax.rem(lax.axis_index("gy") + (offset[1] + n_gy), n_gy),
    )


def remote(sizes, src, dst, send, recv, offset):
    return pltpu.make_async_remote_copy(
        src_ref=src, dst_ref=dst, send_sem=send, recv_sem=recv,
        device_id=at_offset(sizes, offset), device_id_type=pl.DeviceIdType.MESH,
    )


def greet(sizes, offsets):
    barrier = pltpu.get_barrier_semaphore()
    offsets = sorted({(dx % sizes[0], dy % sizes[1]) for dx, dy in offsets})
    for offset in offsets:
        pl.semaphore_signal(
            barrier, inc=1, device_id=at_offset(sizes, offset),
            device_id_type=pl.DeviceIdType.MESH,
        )
    return lambda: pl.semaphore_wait(barrier, len(offsets))


HALO_OFFSETS = [(dx, dy) for dx, dy, _, _, _ in MESSAGES]


def filter_phase(sizes, inputs, scratch, ready):
    (nodes_in, masses_in, cells_in, down_in, along_in) = inputs
    (nodes, masses, cells, down, along, padded, mass_pad, rim_matrix, inner_matrix, states,
     rim_rounded, inner_rounded, sums, sent_x, sent_y, sent_corner, got_x, got_y, got_corner,
     load_sems, send_sems, recv_sems) = scratch

    loads = [
        pltpu.make_async_copy(src, dst, load_sems.at[index])
        for index, (src, dst) in enumerate(
            [(down_in, down), (along_in, along), (cells_in, cells), (masses_in, masses),
             (nodes_in, nodes)]
        )
    ]
    for load in loads:
        load.start()
    loads[0].wait()
    loads[1].wait()

    lanes = lax.broadcasted_iota(jnp.int32, (ROWS, 216), 1)
    to_rows = [one_hot(lanes == down[:, c : c + 1]).astype(BF16) for c in range(2)]
    places = lax.broadcasted_iota(jnp.int32, (216, ROWS), 0)
    to_columns = [one_hot(places == along[c : c + 1, :]).astype(BF16) for c in range(2)]

    loads[2].wait()
    first = dot(to_rows[0], cells[0, 0, 0]).astype(BF16)
    second = dot(to_rows[1], cells[0, 0, 1]).astype(BF16)
    matrix = (dot(first, to_columns[0]) + dot(second, to_columns[1])).astype(BF16)
    rim_matrix[...] = matrix[:, :RIM]
    inner_matrix[...] = matrix[:, RIM:]

    loads[3].wait()
    mass_pad[...] = jnp.zeros(mass_pad.shape, F32)
    for x in range(6):
        high, rest = split(masses[x])
        low, least = split(masses[x] - high.astype(F32))
        mass_pad[8 * x : 8 * x + 6, 0:11] = high.astype(F32)
        mass_pad[8 * x : 8 * x + 6, 16:27] = low.astype(F32)
        mass_pad[8 * x : 8 * x + 6, 32:43] = least.astype(F32)
    pick = one_hot(lax.broadcasted_iota(jnp.int32, (ROWS, 48), 1) == down[:, 2:3]).astype(BF16)
    spread = dot(pick, mass_pad[...].astype(BF16))
    lane = lax.broadcasted_iota(jnp.int32, (ROWS, 128), 1)
    mass = jnp.sum(
        jnp.where(lane % 16 == down[:, 3:4], spread, 0.0), axis=1, keepdims=True
    )
    weight = mass * down[:, 4:5].astype(F32)
    scale1 = 1.0 / (HALF_SPAN * mass)
    shift = CENTER_SHIFT / HALF_SPAN

    loads[4].wait()
    for x in range(6):
        for z in range(11):
            for half in range(2):
                padded[half, 8 * (11 * x + z) : 8 * (11 * x + z) + 6] = nodes[
                    x, z, :, 128 * half : 128 * half + 128
                ].astype(F32)
    for (x, y), start in STARTS.items():
        for half in range(2):
            for low, skip in ((0, 0), (6, 40)):
                states[0, half, start + low : start + low + 6] = padded[
                    half, pl.ds(88 * x + skip + y, 6, stride=8)
                ]
    rim, inner = slice(0, RIM), slice(RIM, ROWS)
    for half in range(2):
        rim_rounded[half] = states[0, half, rim].astype(BF16)
        inner_rounded[half] = states[0, half, inner].astype(BF16)

    buffers = {"x": (sent_x, got_x), "y": (sent_y, got_y), "corner": (sent_corner, got_corner)}

    def moves_of(step, half):
        return [
            remote(
                sizes, buffers[kind][0].at[step, half, here], buffers[kind][1].at[step, half, there],
                send_sems.at[step, half, index], recv_sems.at[step, half, index], (dx, dy),
            )
            for index, (dx, dy, kind, here, there) in enumerate(MESSAGES)
        ]

    def advance(step, half, product, rows):
        if step == 0:
            return product * scale1[rows] - shift * states[0, half, rows]
        return (
            (2.0 * product) * scale1[rows]
            - (2.0 * shift) * states[step, half, rows]
            - states[step - 1, half, rows]
        )

    moves = {}

    def launch(step, half, ahead):
        product = ahead + dot(rim_matrix[rim], rim_rounded[half])
        sums[step, half] = product
        corners = [product[12 * i : 12 * i + 12] for i in range(4)]
        for i in range(4):
            sent_corner[step, half, i] = corners[i]
        sent_x[step, half, 0] = jnp.concatenate([corners[0], corners[2], product[48:96]], axis=0)
        sent_x[step, half, 1] = jnp.concatenate([corners[1], corners[3], product[96:144]], axis=0)
        sent_y[step, half, 0] = jnp.concatenate([product[0:24], product[144:192]], axis=0)
        sent_y[step, half, 1] = jnp.concatenate([product[24:48], product[192:240]], axis=0)
        if step == 0 and half == 0:
            ready()
        moves[step, half] = moves_of(step, half)
        for move in moves[step, half]:
            move.start()

    def inside(step, half):
        inner_next = advance(
            step,
            half,
            dot(rim_matrix[inner], rim_rounded[half])
            + dot(inner_matrix[inner], inner_rounded[half]),
            inner,
        )
        states[step + 1, half, inner] = inner_next
        if step == FILTER_DEG - 1:
            return inner_next
        inner_rounded[half] = inner_next.astype(BF16)
        return dot(inner_matrix[rim], inner_rounded[half])

    def finish(step, half):
        for move in moves[step, half]:
            move.wait_recv()
        own = sums[step, half]
        x0, x5 = got_x[step, half, 0], got_x[step, half, 1]
        y0, y5 = got_y[step, half, 0], got_y[step, half, 1]
        far = [got_corner[step, half, i] for i in range(4)]
        theirs = jnp.concatenate(
            [
                x0[0:12] + y0[0:12] + far[0],
                x5[0:12] + y0[12:24] + far[1],
                x0[12:24] + y5[0:12] + far[2],
                x5[12:24] + y5[12:24] + far[3],
                x0[24:72],
                x5[24:72],
                y0[24:72],
                y5[24:72],
            ],
            axis=0,
        )
        rim_next = advance(step, half, own + theirs, rim)
        states[step + 1, half, rim] = rim_next
        rim_rounded[half] = rim_next.astype(BF16)
        return rim_next

    for half in range(2):
        launch(0, half, dot(inner_matrix[rim], inner_rounded[half]))
    ahead = [inside(0, half) for half in range(2)]
    for step in range(FILTER_DEG - 1):
        for half in range(2):
            finish(step, half)
            launch(step + 1, half, ahead[half])
            ahead[half] = inside(step + 1, half)
    grams = gram(jnp.concatenate(ahead, axis=1), weight[inner])
    keep = lambda a: jnp.concatenate([a[0:24], a[48:96], a[144:192]], axis=0)
    rims = [keep(finish(FILTER_DEG - 1, half)) for half in range(2)]
    rim_grams = gram(jnp.concatenate(rims, axis=1), keep(weight[rim]))
    return tuple(a + b for a, b in zip(grams, rim_grams)), sum(moves.values(), [])


def whole_rows(states):
    return jnp.concatenate([states[FILTER_DEG, 0], states[FILTER_DEG, 1]], axis=1)


def rotate_phase(filtered, factor, padded, out):
    result = dot3(filtered, factor)
    for (x, y), start in STARTS.items():
        for half in range(2):
            lanes = slice(128 * half, 128 * half + 128)
            padded[half, pl.ds(88 * x + y, 6, stride=8)] = result[start : start + 6, lanes]
            padded[half, pl.ds(88 * x + 48 + y, 5, stride=8)] = result[
                start + 7 : start + 12, lanes
            ]
    for x in range(6):
        for z in range(11):
            low = 8 * (11 * x + z)
            out[x, z] = jnp.concatenate(
                [padded[0, low : low + 6], padded[1, low : low + 6]], axis=1
            ).astype(BF16)


def fused_kernel(sizes, node_total, *refs):
    inputs, out, scratch, extra = refs[:5], refs[5], refs[6:28], refs[28:]
    (own, row_in, part, column_in, whole,
     row_send, row_recv, col_send, col_recv, all_send, all_recv) = extra
    n_gx, n_gy = sizes
    my_y = lax.axis_index("gy")
    ready = greet(
        sizes,
        HALO_OFFSETS + [(0, d) for d in range(1, n_gy)] + [(d, 0) for d in range(1, n_gx)],
    )
    grams, moves = filter_phase(sizes, inputs, scratch, ready)
    pieces, height = own.shape[0], own.shape[2]
    stacked = jnp.concatenate(grams, axis=0)
    row_moves, col_moves, all_moves = [], [], []
    for p in range(pieces):
        for index in range(n_gy):
            low = (index * pieces + p) * height
            own[p, index] = stacked[low : low + height]
        row_moves.append([
            remote(sizes, own.at[p, lax.rem(my_y + d, n_gy)], row_in.at[p, d - 1],
                   row_send.at[p, d - 1], row_recv.at[p, d - 1], (0, d))
            for d in range(1, n_gy)
        ])
        for move in row_moves[p]:
            move.start()
        col_moves.append([
            remote(sizes, part.at[p], column_in.at[p, d - 1],
                   col_send.at[p, d - 1], col_recv.at[p, d - 1], (d, 0))
            for d in range(1, n_gx)
        ])
        all_moves.append([
            remote(sizes, whole.at[p, my_y], whole.at[p, my_y],
                   all_send.at[p, d - 1], all_recv.at[p, d - 1], (0, d))
            for d in range(1, n_gy)
        ])

    def second(p):
        for move in row_moves[p]:
            move.wait_recv()
        total = own[p, my_y]
        for d in range(1, n_gy):
            total = total + row_in[p, d - 1]
        part[p] = total
        for move in col_moves[p]:
            move.start()

    def third(p):
        for move in col_moves[p]:
            move.wait_recv()
        total = part[p]
        for d in range(1, n_gx):
            total = total + column_in[p, d - 1]
        whole[p, my_y] = total
        for move in all_moves[p]:
            move.start()

    for p in range(pieces):
        second(p)
        if p >= 1:
            third(p - 1)
    third(pieces - 1)
    for p in range(pieces):
        for move in all_moves[p]:
            move.wait_recv()
    stacked = jnp.concatenate(
        [whole[p, index] for index in range(n_gy) for p in range(pieces)], axis=0
    )
    factor = inverse_root(stacked, node_total)
    rotate_phase(whole_rows(scratch[9]), factor, scratch[5], out)
    for move in moves + sum(row_moves + col_moves + all_moves, []):
        move.wait_send()


def filter_kernel(sizes, *refs):
    inputs, filtered, stacked, scratch = refs[:5], refs[5], refs[6], refs[7:]
    grams, moves = filter_phase(sizes, inputs, scratch, greet(sizes, HALO_OFFSETS))
    stacked[...] = jnp.concatenate(grams, axis=0)
    filtered[...] = whole_rows(scratch[9])
    for move in moves:
        move.wait_send()


def rotate_kernel(node_total, filtered, stacked, out, padded):
    rotate_phase(filtered[...], inverse_root(stacked[...], node_total), padded, out)


def body(orbitals, masses, cell_matrices):
    n_gx, n_gy = lax.axis_size("gx"), lax.axis_size("gy")
    sizes = (n_gx, n_gy)
    assert orbitals.shape == (6, 6, 11, 256) and cell_matrices.shape == (1, 1, 2, 216, 216)
    node_total = 5 * n_gx * 5 * n_gy * 11
    nodes = jnp.transpose(orbitals, (0, 2, 1, 3))
    down, along = tables()
    arguments = (nodes, masses, cell_matrices, jnp.asarray(down), jnp.asarray(along))
    vmem = pl.BlockSpec(memory_space=pltpu.VMEM)
    hbm = pl.BlockSpec(memory_space=pltpu.MemorySpace.HBM)
    filter_scratch = [
        pltpu.VMEM(nodes.shape, BF16),
        pltpu.VMEM(masses.shape, F32),
        pltpu.VMEM(cell_matrices.shape, BF16),
        pltpu.VMEM(down.shape, jnp.int32),
        pltpu.VMEM(along.shape, jnp.int32),
        pltpu.VMEM((2, 528, 128), F32),
        pltpu.VMEM((48, 128), F32),
        pltpu.VMEM((ROWS, RIM), BF16),
        pltpu.VMEM((ROWS, INNER), BF16),
        pltpu.VMEM((FILTER_DEG + 1, 2, ROWS, 128), F32),
        pltpu.VMEM((2, RIM, 128), BF16),
        pltpu.VMEM((2, INNER, 128), BF16),
        pltpu.VMEM((FILTER_DEG, 2, RIM, 128), F32),
    ]
    filter_scratch += [
        pltpu.VMEM((FILTER_DEG, 2) + shape + (128,), F32)
        for shape in ((2, 72), (2, 72), (4, 12)) * 2
    ]
    filter_scratch += [
        pltpu.SemaphoreType.DMA((5,)),
        pltpu.SemaphoreType.DMA((FILTER_DEG, 2, len(MESSAGES))),
        pltpu.SemaphoreType.DMA((FILTER_DEG, 2, len(MESSAGES))),
    ]
    params = pltpu.CompilerParams(
        collective_id=0, has_side_effects=True, vmem_limit_bytes=VMEM_BYTES
    )
    if 384 % (8 * PIECES * n_gy) == 0:
        height = 384 // n_gy // PIECES
        result = pl.pallas_call(
            functools.partial(fused_kernel, sizes, node_total),
            out_shape=jax.ShapeDtypeStruct(nodes.shape, BF16),
            in_specs=[hbm] * 5,
            out_specs=vmem,
            scratch_shapes=filter_scratch
            + [
                pltpu.VMEM((PIECES, n_gy, height, 128), F32),
                pltpu.VMEM((PIECES, n_gy - 1, height, 128), F32),
                pltpu.VMEM((PIECES, height, 128), F32),
                pltpu.VMEM((PIECES, n_gx - 1, height, 128), F32),
                pltpu.VMEM((PIECES, n_gy, height, 128), F32),
            ]
            + [pltpu.SemaphoreType.DMA((PIECES, n - 1)) for n in (n_gy, n_gy, n_gx, n_gx, n_gy, n_gy)],
            compiler_params=params,
        )(*arguments)
    else:
        filtered, stacked = pl.pallas_call(
            functools.partial(filter_kernel, sizes),
            out_shape=[
                jax.ShapeDtypeStruct((ROWS, 256), F32),
                jax.ShapeDtypeStruct((384, 128), F32),
            ],
            in_specs=[hbm] * 5,
            out_specs=[vmem] * 2,
            scratch_shapes=filter_scratch,
            compiler_params=params,
        )(*arguments)
        stacked = lax.psum(stacked, ("gx", "gy"))
        result = pl.pallas_call(
            functools.partial(rotate_kernel, node_total),
            out_shape=jax.ShapeDtypeStruct(nodes.shape, BF16),
            in_specs=[vmem] * 2,
            out_specs=vmem,
            scratch_shapes=[pltpu.VMEM((2, 528, 128), F32)],
            compiler_params=pltpu.CompilerParams(vmem_limit_bytes=VMEM_BYTES),
        )(filtered, stacked)
    return jnp.transpose(result, (0, 2, 1, 3))


def solution(mesh):
    return jax.shard_map(
        body,
        mesh=mesh,
        in_specs=(P("gx", "gy", None, None), P("gx", "gy", None), P("gx", "gy", None, None, None)),
        out_specs=P("gx", "gy", None, None),
        check_vma=False,
    )
```

```python
import functools

import jax
import jax.numpy as jnp
import numpy as np
from jax import lax
from jax.experimental import pallas as pl
from jax.experimental.pallas import tpu as pltpu
from jax.sharding import PartitionSpec as P

FILTER_DEG = 3
CENTER_SHIFT = 12.0
HALF_SPAN = 12.0

RIM = 240
ROWS = 432
INNER = ROWS - RIM
CORNERS = 48
PIECES = 1
VMEM_BYTES = (64 << 20) - (128 << 10)
BF16 = jnp.bfloat16
F32 = jnp.float32

MESSAGES = (
    (-1, -1, "corner", 0, 3),
    (1, -1, "corner", 1, 2),
    (-1, 1, "corner", 2, 1),
    (1, 1, "corner", 3, 0),
    (-1, 0, "x", 0, 1),
    (1, 0, "x", 1, 0),
    (0, -1, "y", 0, 1),
    (0, 1, "y", 1, 0),
)


def column_starts():
    starts = {(0, 0): 0, (5, 0): 12, (0, 5): 24, (5, 5): 36}
    for i in range(4):
        starts[(0, i + 1)] = 48 + 12 * i
        starts[(5, i + 1)] = 96 + 12 * i
        starts[(i + 1, 0)] = 144 + 12 * i
        starts[(i + 1, 5)] = 192 + 12 * i
    for i in range(4):
        for j in range(4):
            starts[(i + 1, j + 1)] = RIM + 12 * (4 * i + j)
    return starts


STARTS = column_starts()


def tables():
    down = np.zeros((ROWS, 128), np.int32)
    along = np.full((8, ROWS), -1, np.int32)
    for (x, y), start in STARTS.items():
        for half in range(2):
            for k in range(6):
                row, z = start + 6 * half + k, 5 * half + k
                for cell in range(2):
                    inside = 0 <= z - 5 * cell <= 5
                    down[row, cell] = (x * 6 + y) * 6 + z - 5 * cell if inside else -1
                down[row, 2], down[row, 3] = 8 * x + y, z
                down[row, 4] = int(x < 5 and y < 5 and not (half == 1 and k == 0))
                along[half, row] = (x * 6 + y) * 6 + k
    return down, along


def dot(a, b):
    return jnp.dot(a, b, preferred_element_type=F32)


def dot_rows(a, b):
    return lax.dot_general(a, b, (((0,), (0,)), ((), ())), preferred_element_type=F32)


def split(a):
    high = a.astype(BF16)
    return high, (a - high.astype(F32)).astype(BF16)


def dot3(a, b):
    a_high, a_low = split(a)
    b_high, b_low = split(b)
    return dot(a_high, b_high) + (dot(a_high, b_low) + dot(a_low, b_high))


def one_hot(condition):
    return jnp.where(condition, 1.0, 0.0).astype(F32)


def gram(rows, weight):
    a_high, a_low = split(rows * weight)
    b_high, b_low = split(rows)

    def part(lanes, columns):
        return dot_rows(a_high[:, lanes], b_high[:, columns]) + (
            dot_rows(a_high[:, lanes], b_low[:, columns])
            + dot_rows(a_low[:, lanes], b_high[:, columns])
        )

    top = part(slice(0, 128), slice(0, 256))
    return top[:, :128], top[:, 128:], part(slice(128, 256), slice(128, 256))


def block_ids():
    return (
        lax.broadcasted_iota(jnp.int32, (128, 128), 0),
        lax.broadcasted_iota(jnp.int32, (128, 128), 1),
    )


def pack(grams):
    s00, s01, s11 = grams
    row, col = block_ids()
    diagonal = jnp.sum(jnp.where(row == col, s11, 0.0), axis=0, keepdims=True)
    return jnp.concatenate([s01, jnp.where(row <= col, s00, s11)], axis=0), diagonal


def unpack(packed, diagonal):
    s01, both = packed[0:128], packed[128:256]
    row, col = block_ids()
    upper = jnp.where(row <= col, both, 0.0)
    lower = jnp.where(row > col, both, 0.0)
    s00 = upper + jnp.where(row < col, both, 0.0).T
    s11 = lower + lower.T + jnp.where(row == col, diagonal, 0.0)
    return jnp.concatenate([s00, s01, s11], axis=0)


def inverse_root(stacked, node_total):
    s00, s01, s11 = stacked[0:128], stacked[128:256], stacked[256:384]
    top = jnp.concatenate([s00, s01], axis=1)
    bottom = jnp.concatenate([s01.T, s11], axis=1)
    inter = jnp.concatenate([top, bottom], axis=0) * (1.0 / node_total)
    frob2 = jnp.sum(jnp.sum(inter * inter, axis=1, keepdims=True), axis=0, keepdims=True)
    frob = jnp.sqrt(frob2)
    current = inter / frob
    row_id = lax.broadcasted_iota(jnp.int32, (256, 256), 0)
    col_id = lax.broadcasted_iota(jnp.int32, (256, 256), 1)
    identity = one_hot(row_id == col_id)
    square = dot3(current, current)
    tail = 1.6875 * identity - 0.5625 * current + 0.0625 * square
    factor_z = 2.25 * identity - 2.4375 * current + dot3(square, tail)
    return factor_z / jnp.sqrt(frob)


def at_offset(sizes, offset):
    n_gx, n_gy = sizes
    return (
        lax.rem(lax.axis_index("gx") + (offset[0] + n_gx), n_gx),
        lax.rem(lax.axis_index("gy") + (offset[1] + n_gy), n_gy),
    )


def remote(sizes, src, dst, send, recv, offset):
    return pltpu.make_async_remote_copy(
        src_ref=src, dst_ref=dst, send_sem=send, recv_sem=recv,
        device_id=at_offset(sizes, offset), device_id_type=pl.DeviceIdType.MESH,
    )


def greet(sizes, offsets):
    barrier = pltpu.get_barrier_semaphore()
    offsets = sorted({(dx % sizes[0], dy % sizes[1]) for dx, dy in offsets})
    for offset in offsets:
        pl.semaphore_signal(
            barrier, inc=1, device_id=at_offset(sizes, offset),
            device_id_type=pl.DeviceIdType.MESH,
        )
    return lambda: pl.semaphore_wait(barrier, len(offsets))


HALO_OFFSETS = [(dx, dy) for dx, dy, _, _, _ in MESSAGES]


def filter_phase(sizes, inputs, scratch, ready):
    (nodes_in, masses_in, cells_in, down_in, along_in) = inputs
    (nodes, masses, cells, down, along, padded, mass_pad, rim_matrix, inner_matrix, states,
     rim_rounded, inner_rounded, sums, sent_x, sent_y, sent_corner, got_x, got_y, got_corner,
     load_sems, send_sems, recv_sems) = scratch

    loads = [
        pltpu.make_async_copy(src, dst, load_sems.at[index])
        for index, (src, dst) in enumerate(
            [(down_in, down), (along_in, along), (cells_in, cells), (masses_in, masses),
             (nodes_in, nodes)]
        )
    ]
    for load in loads:
        load.start()
    loads[0].wait()
    loads[1].wait()

    lanes = lax.broadcasted_iota(jnp.int32, (ROWS, 216), 1)
    to_rows = [one_hot(lanes == down[:, c : c + 1]).astype(BF16) for c in range(2)]
    places = lax.broadcasted_iota(jnp.int32, (216, ROWS), 0)
    to_columns = [one_hot(places == along[c : c + 1, :]).astype(BF16) for c in range(2)]

    loads[2].wait()
    first = dot(to_rows[0], cells[0, 0, 0]).astype(BF16)
    second = dot(to_rows[1], cells[0, 0, 1]).astype(BF16)
    matrix = (dot(first, to_columns[0]) + dot(second, to_columns[1])).astype(BF16)
    rim_matrix[...] = matrix[:, :RIM]
    inner_matrix[...] = matrix[:, RIM:]

    loads[3].wait()
    mass_pad[...] = jnp.zeros(mass_pad.shape, F32)
    for x in range(6):
        high, rest = split(masses[x])
        low, least = split(masses[x] - high.astype(F32))
        mass_pad[8 * x : 8 * x + 6, 0:11] = high.astype(F32)
        mass_pad[8 * x : 8 * x + 6, 16:27] = low.astype(F32)
        mass_pad[8 * x : 8 * x + 6, 32:43] = least.astype(F32)
    pick = one_hot(lax.broadcasted_iota(jnp.int32, (ROWS, 48), 1) == down[:, 2:3]).astype(BF16)
    spread = dot(pick, mass_pad[...].astype(BF16))
    lane = lax.broadcasted_iota(jnp.int32, (ROWS, 128), 1)
    mass = jnp.sum(
        jnp.where(lane % 16 == down[:, 3:4], spread, 0.0), axis=1, keepdims=True
    )
    weight = mass * down[:, 4:5].astype(F32)
    scale1 = 1.0 / (HALF_SPAN * mass)
    shift = CENTER_SHIFT / HALF_SPAN

    loads[4].wait()
    for x in range(6):
        for z in range(11):
            for half in range(2):
                padded[half, 8 * (11 * x + z) : 8 * (11 * x + z) + 6] = nodes[
                    x, z, :, 128 * half : 128 * half + 128
                ].astype(F32)
    for (x, y), start in STARTS.items():
        for half in range(2):
            for low, skip in ((0, 0), (6, 40)):
                states[0, half, start + low : start + low + 6] = padded[
                    half, pl.ds(88 * x + skip + y, 6, stride=8)
                ]
    rim, inner = slice(0, RIM), slice(RIM, ROWS)
    for half in range(2):
        rim_rounded[half] = states[0, half, rim].astype(BF16)
        inner_rounded[half] = states[0, half, inner].astype(BF16)

    buffers = {"x": (sent_x, got_x), "y": (sent_y, got_y), "corner": (sent_corner, got_corner)}

    def moves_of(step, half):
        return [
            remote(
                sizes, buffers[kind][0].at[step, half, here], buffers[kind][1].at[step, half, there],
                send_sems.at[step, half, index], recv_sems.at[step, half, index], (dx, dy),
            )
            for index, (dx, dy, kind, here, there) in enumerate(MESSAGES)
        ]

    def advance(step, half, product, rows):
        if step == 0:
            return product * scale1[rows] - shift * states[0, half, rows]
        return (
            (2.0 * product) * scale1[rows]
            - (2.0 * shift) * states[step, half, rows]
            - states[step - 1, half, rows]
        )

    moves = {}

    def launch(step, half, ahead):
        product = ahead + dot(rim_matrix[rim], rim_rounded[half])
        sums[step, half] = product
        corners = [product[12 * i : 12 * i + 12] for i in range(4)]
        for i in range(4):
            sent_corner[step, half, i] = corners[i]
        sent_x[step, half, 0] = jnp.concatenate([corners[0], corners[2], product[48:96]], axis=0)
        sent_x[step, half, 1] = jnp.concatenate([corners[1], corners[3], product[96:144]], axis=0)
        sent_y[step, half, 0] = jnp.concatenate([product[0:24], product[144:192]], axis=0)
        sent_y[step, half, 1] = jnp.concatenate([product[24:48], product[192:240]], axis=0)
        if step == 0 and half == 0:
            ready()
        moves[step, half] = moves_of(step, half)
        for move in moves[step, half]:
            move.start()

    def inside(step, half):
        inner_next = advance(
            step,
            half,
            dot(rim_matrix[inner], rim_rounded[half])
            + dot(inner_matrix[inner], inner_rounded[half]),
            inner,
        )
        states[step + 1, half, inner] = inner_next
        if step == FILTER_DEG - 1:
            return inner_next
        inner_rounded[half] = inner_next.astype(BF16)
        return dot(inner_matrix[rim], inner_rounded[half])

    def finish(step, half):
        for move in moves[step, half]:
            move.wait_recv()
        own = sums[step, half]
        x0, x5 = got_x[step, half, 0], got_x[step, half, 1]
        y0, y5 = got_y[step, half, 0], got_y[step, half, 1]
        far = [got_corner[step, half, i] for i in range(4)]
        theirs = jnp.concatenate(
            [
                x0[0:12] + y0[0:12] + far[0],
                x5[0:12] + y0[12:24] + far[1],
                x0[12:24] + y5[0:12] + far[2],
                x5[12:24] + y5[12:24] + far[3],
                x0[24:72],
                x5[24:72],
                y0[24:72],
                y5[24:72],
            ],
            axis=0,
        )
        rim_next = advance(step, half, own + theirs, rim)
        states[step + 1, half, rim] = rim_next
        rim_rounded[half] = rim_next.astype(BF16)
        return rim_next

    for half in range(2):
        launch(0, half, dot(inner_matrix[rim], inner_rounded[half]))
    ahead = [inside(0, half) for half in range(2)]
    for step in range(FILTER_DEG - 1):
        for half in range(2):
            finish(step, half)
            launch(step + 1, half, ahead[half])
            ahead[half] = inside(step + 1, half)
    grams = gram(jnp.concatenate(ahead, axis=1), weight[inner])
    keep = lambda a: jnp.concatenate([a[0:24], a[48:96], a[144:192]], axis=0)
    rims = [keep(finish(FILTER_DEG - 1, half)) for half in range(2)]
    rim_grams = gram(jnp.concatenate(rims, axis=1), keep(weight[rim]))
    return tuple(a + b for a, b in zip(grams, rim_grams)), sum(moves.values(), [])


def whole_rows(states):
    return jnp.concatenate([states[FILTER_DEG, 0], states[FILTER_DEG, 1]], axis=1)


def rotate_phase(filtered, factor, padded, out):
    result = dot3(filtered, factor)
    for (x, y), start in STARTS.items():
        for half in range(2):
            lanes = slice(128 * half, 128 * half + 128)
            padded[half, pl.ds(88 * x + y, 6, stride=8)] = result[start : start + 6, lanes]
            padded[half, pl.ds(88 * x + 48 + y, 5, stride=8)] = result[
                start + 7 : start + 12, lanes
            ]
    for x in range(6):
        for z in range(11):
            low = 8 * (11 * x + z)
            out[x, z] = jnp.concatenate(
                [padded[0, low : low + 6], padded[1, low : low + 6]], axis=1
            ).astype(BF16)


def fused_kernel(sizes, node_total, *refs):
    inputs, out, scratch, extra = refs[:5], refs[5], refs[6:28], refs[28:]
    (own, row_in, part, column_in, whole,
     row_send, row_recv, col_send, col_recv, all_send, all_recv) = extra
    n_gx, n_gy = sizes
    my_y = lax.axis_index("gy")
    ready = greet(
        sizes,
        HALO_OFFSETS + [(0, d) for d in range(1, n_gy)] + [(d, 0) for d in range(1, n_gx)],
    )
    grams, moves = filter_phase(sizes, inputs, scratch, ready)
    pieces, height = own.shape[0], own.shape[2] - 1
    packed, diagonal = pack(grams)
    row_moves, col_moves, all_moves = [], [], []
    for p in range(pieces):
        for index in range(n_gy):
            low = (index * pieces + p) * height
            own[p, index, 0:height] = packed[low : low + height]
            own[p, index, height : height + 1] = diagonal
        row_moves.append([
            remote(sizes, own.at[p, lax.rem(my_y + d, n_gy)], row_in.at[p, d - 1],
                   row_send.at[p, d - 1], row_recv.at[p, d - 1], (0, d))
            for d in range(1, n_gy)
        ])
        for move in row_moves[p]:
            move.start()
        col_moves.append([
            remote(sizes, part.at[p], column_in.at[p, d - 1],
                   col_send.at[p, d - 1], col_recv.at[p, d - 1], (d, 0))
            for d in range(1, n_gx)
        ])
        all_moves.append([
            remote(sizes, whole.at[p, my_y], whole.at[p, my_y],
                   all_send.at[p, d - 1], all_recv.at[p, d - 1], (0, d))
            for d in range(1, n_gy)
        ])

    def second(p):
        for move in row_moves[p]:
            move.wait_recv()
        total = own[p, my_y]
        for d in range(1, n_gy):
            total = total + row_in[p, d - 1]
        part[p] = total
        for move in col_moves[p]:
            move.start()

    def third(p):
        for move in col_moves[p]:
            move.wait_recv()
        total = part[p]
        for d in range(1, n_gx):
            total = total + column_in[p, d - 1]
        whole[p, my_y] = total
        for move in all_moves[p]:
            move.start()

    for p in range(pieces):
        second(p)
        if p >= 1:
            third(p - 1)
    third(pieces - 1)
    for p in range(pieces):
        for move in all_moves[p]:
            move.wait_recv()
    packed = jnp.concatenate(
        [whole[p, index, 0:height] for index in range(n_gy) for p in range(pieces)], axis=0
    )
    stacked = unpack(packed, whole[0, 0, height : height + 1])
    factor = inverse_root(stacked, node_total)
    rotate_phase(whole_rows(scratch[9]), factor, scratch[5], out)
    for move in moves + sum(row_moves + col_moves + all_moves, []):
        move.wait_send()


def filter_kernel(sizes, *refs):
    inputs, filtered, stacked, scratch = refs[:5], refs[5], refs[6], refs[7:]
    grams, moves = filter_phase(sizes, inputs, scratch, greet(sizes, HALO_OFFSETS))
    stacked[...] = jnp.concatenate(grams, axis=0)
    filtered[...] = whole_rows(scratch[9])
    for move in moves:
        move.wait_send()


def rotate_kernel(node_total, filtered, stacked, out, padded):
    rotate_phase(filtered[...], inverse_root(stacked[...], node_total), padded, out)


def body(orbitals, masses, cell_matrices):
    n_gx, n_gy = lax.axis_size("gx"), lax.axis_size("gy")
    sizes = (n_gx, n_gy)
    assert orbitals.shape == (6, 6, 11, 256) and cell_matrices.shape == (1, 1, 2, 216, 216)
    node_total = 5 * n_gx * 5 * n_gy * 11
    nodes = jnp.transpose(orbitals, (0, 2, 1, 3))
    down, along = tables()
    arguments = (nodes, masses, cell_matrices, jnp.asarray(down), jnp.asarray(along))
    vmem = pl.BlockSpec(memory_space=pltpu.VMEM)
    hbm = pl.BlockSpec(memory_space=pltpu.MemorySpace.HBM)
    filter_scratch = [
        pltpu.VMEM(nodes.shape, BF16),
        pltpu.VMEM(masses.shape, F32),
        pltpu.VMEM(cell_matrices.shape, BF16),
        pltpu.VMEM(down.shape, jnp.int32),
        pltpu.VMEM(along.shape, jnp.int32),
        pltpu.VMEM((2, 528, 128), F32),
        pltpu.VMEM((48, 128), F32),
        pltpu.VMEM((ROWS, RIM), BF16),
        pltpu.VMEM((ROWS, INNER), BF16),
        pltpu.VMEM((FILTER_DEG + 1, 2, ROWS, 128), F32),
        pltpu.VMEM((2, RIM, 128), BF16),
        pltpu.VMEM((2, INNER, 128), BF16),
        pltpu.VMEM((FILTER_DEG, 2, RIM, 128), F32),
    ]
    filter_scratch += [
        pltpu.VMEM((FILTER_DEG, 2) + shape + (128,), F32)
        for shape in ((2, 72), (2, 72), (4, 12)) * 2
    ]
    filter_scratch += [
        pltpu.SemaphoreType.DMA((5,)),
        pltpu.SemaphoreType.DMA((FILTER_DEG, 2, len(MESSAGES))),
        pltpu.SemaphoreType.DMA((FILTER_DEG, 2, len(MESSAGES))),
    ]
    params = pltpu.CompilerParams(
        collective_id=0, has_side_effects=True, vmem_limit_bytes=VMEM_BYTES
    )
    if 256 % (8 * PIECES * n_gy) == 0:
        height = 256 // n_gy // PIECES + 1
        result = pl.pallas_call(
            functools.partial(fused_kernel, sizes, node_total),
            out_shape=jax.ShapeDtypeStruct(nodes.shape, BF16),
            in_specs=[hbm] * 5,
            out_specs=vmem,
            scratch_shapes=filter_scratch
            + [
                pltpu.VMEM((PIECES, n_gy, height, 128), F32),
                pltpu.VMEM((PIECES, n_gy - 1, height, 128), F32),
                pltpu.VMEM((PIECES, height, 128), F32),
                pltpu.VMEM((PIECES, n_gx - 1, height, 128), F32),
                pltpu.VMEM((PIECES, n_gy, height, 128), F32),
            ]
            + [pltpu.SemaphoreType.DMA((PIECES, n - 1)) for n in (n_gy, n_gy, n_gx, n_gx, n_gy, n_gy)],
            compiler_params=params,
        )(*arguments)
    else:
        filtered, stacked = pl.pallas_call(
            functools.partial(filter_kernel, sizes),
            out_shape=[
                jax.ShapeDtypeStruct((ROWS, 256), F32),
                jax.ShapeDtypeStruct((384, 128), F32),
            ],
            in_specs=[hbm] * 5,
            out_specs=[vmem] * 2,
            scratch_shapes=filter_scratch,
            compiler_params=params,
        )(*arguments)
        stacked = lax.psum(stacked, ("gx", "gy"))
        result = pl.pallas_call(
            functools.partial(rotate_kernel, node_total),
            out_shape=jax.ShapeDtypeStruct(nodes.shape, BF16),
            in_specs=[vmem] * 2,
            out_specs=vmem,
            scratch_shapes=[pltpu.VMEM((2, 528, 128), F32)],
            compiler_params=pltpu.CompilerParams(vmem_limit_bytes=VMEM_BYTES),
        )(filtered, stacked)
    return jnp.transpose(result, (0, 2, 1, 3))


def solution(mesh):
    return jax.shard_map(
        body,
        mesh=mesh,
        in_specs=(P("gx", "gy", None, None), P("gx", "gy", None), P("gx", "gy", None, None, None)),
        out_specs=P("gx", "gy", None, None),
        check_vma=False,
    )
```

```python
import functools

import jax
import jax.numpy as jnp
import numpy as np
from jax import lax
from jax.experimental import pallas as pl
from jax.experimental.pallas import tpu as pltpu
from jax.sharding import PartitionSpec as P

FILTER_DEG = 3
CENTER_SHIFT = 12.0
HALF_SPAN = 12.0

RIM = 240
ROWS = 432
INNER = ROWS - RIM
CORNERS = 48
PIECES = 1
VMEM_BYTES = (64 << 20) - (128 << 10)
BF16 = jnp.bfloat16
F32 = jnp.float32

MESSAGES = (
    (-1, -1, "corner", 0, 3),
    (1, -1, "corner", 1, 2),
    (-1, 1, "corner", 2, 1),
    (1, 1, "corner", 3, 0),
    (-1, 0, "x", 0, 1),
    (1, 0, "x", 1, 0),
    (0, -1, "y", 0, 1),
    (0, 1, "y", 1, 0),
)


def column_starts():
    starts = {(0, 0): 0, (5, 0): 12, (0, 5): 24, (5, 5): 36}
    for i in range(4):
        starts[(0, i + 1)] = 48 + 12 * i
        starts[(5, i + 1)] = 96 + 12 * i
        starts[(i + 1, 0)] = 144 + 12 * i
        starts[(i + 1, 5)] = 192 + 12 * i
    for i in range(4):
        for j in range(4):
            starts[(i + 1, j + 1)] = RIM + 12 * (4 * i + j)
    return starts


STARTS = column_starts()


def tables():
    down = np.zeros((ROWS, 128), np.int32)
    along = np.full((8, ROWS), -1, np.int32)
    for (x, y), start in STARTS.items():
        for half in range(2):
            for k in range(6):
                row, z = start + 6 * half + k, 5 * half + k
                for cell in range(2):
                    inside = 0 <= z - 5 * cell <= 5
                    down[row, cell] = (x * 6 + y) * 6 + z - 5 * cell if inside else -1
                down[row, 2], down[row, 3] = 8 * x + y, z
                down[row, 4] = int(x < 5 and y < 5 and not (half == 1 and k == 0))
                along[half, row] = (x * 6 + y) * 6 + k
    return down, along


def dot(a, b):
    return jnp.dot(a, b, preferred_element_type=F32)


def dot_rows(a, b):
    return lax.dot_general(a, b, (((0,), (0,)), ((), ())), preferred_element_type=F32)


def split(a):
    high = a.astype(BF16)
    return high, (a - high.astype(F32)).astype(BF16)


def dot3(a, b):
    a_high, a_low = split(a)
    b_high, b_low = split(b)
    return dot(a_high, b_high) + (dot(a_high, b_low) + dot(a_low, b_high))


def one_hot(condition):
    return jnp.where(condition, 1.0, 0.0).astype(F32)


def gram(rows, weight):
    a_high, a_low = split(rows * weight)
    b_high, b_low = split(rows)

    def part(lanes, columns):
        return dot_rows(a_high[:, lanes], b_high[:, columns]) + (
            dot_rows(a_high[:, lanes], b_low[:, columns])
            + dot_rows(a_low[:, lanes], b_high[:, columns])
        )

    top = part(slice(0, 128), slice(0, 256))
    return top[:, :128], top[:, 128:], part(slice(128, 256), slice(128, 256))


def block_ids():
    return (
        lax.broadcasted_iota(jnp.int32, (128, 128), 0),
        lax.broadcasted_iota(jnp.int32, (128, 128), 1),
    )


def pack(grams):
    s00, s01, s11 = grams
    row, col = block_ids()
    diagonal = jnp.sum(jnp.where(row == col, s11, 0.0), axis=0, keepdims=True)
    return jnp.concatenate([s01, jnp.where(row <= col, s00, s11)], axis=0), diagonal


def unpack(packed, diagonal):
    s01, both = packed[0:128], packed[128:256]
    row, col = block_ids()
    upper = jnp.where(row <= col, both, 0.0)
    lower = jnp.where(row > col, both, 0.0)
    s00 = upper + jnp.where(row < col, both, 0.0).T
    s11 = lower + lower.T + jnp.where(row == col, diagonal, 0.0)
    return jnp.concatenate([s00, s01, s11], axis=0)


def inverse_root(stacked, node_total):
    s00, s01, s11 = stacked[0:128], stacked[128:256], stacked[256:384]
    top = jnp.concatenate([s00, s01], axis=1)
    bottom = jnp.concatenate([s01.T, s11], axis=1)
    inter = jnp.concatenate([top, bottom], axis=0) * (1.0 / node_total)
    frob2 = jnp.sum(jnp.sum(inter * inter, axis=1, keepdims=True), axis=0, keepdims=True)
    frob = jnp.sqrt(frob2)
    current = inter / frob
    row_id = lax.broadcasted_iota(jnp.int32, (256, 256), 0)
    col_id = lax.broadcasted_iota(jnp.int32, (256, 256), 1)
    identity = one_hot(row_id == col_id)
    square = dot3(current, current)
    tail = 1.6875 * identity - 0.5625 * current + 0.0625 * square
    factor_z = 2.25 * identity - 2.4375 * current + dot3(square, tail)
    return factor_z / jnp.sqrt(frob)


def at_offset(sizes, offset):
    n_gx, n_gy = sizes
    return (
        lax.rem(lax.axis_index("gx") + (offset[0] + n_gx), n_gx),
        lax.rem(lax.axis_index("gy") + (offset[1] + n_gy), n_gy),
    )


def remote(sizes, src, dst, send, recv, offset):
    return pltpu.make_async_remote_copy(
        src_ref=src, dst_ref=dst, send_sem=send, recv_sem=recv,
        device_id=at_offset(sizes, offset), device_id_type=pl.DeviceIdType.MESH,
    )


def greet(sizes, offsets):
    barrier = pltpu.get_barrier_semaphore()
    offsets = sorted({(dx % sizes[0], dy % sizes[1]) for dx, dy in offsets})
    for offset in offsets:
        pl.semaphore_signal(
            barrier, inc=1, device_id=at_offset(sizes, offset),
            device_id_type=pl.DeviceIdType.MESH,
        )
    return lambda: pl.semaphore_wait(barrier, len(offsets))


HALO_OFFSETS = [(dx, dy) for dx, dy, _, _, _ in MESSAGES]


def filter_phase(sizes, inputs, scratch, ready):
    (nodes_in, masses_in, cells_in, down_in, along_in) = inputs
    (nodes, masses, cells, down, along, padded, mass_pad, rim_matrix, inner_matrix, states,
     rim_rounded, inner_rounded, sums, sent_x, sent_y, sent_corner, got_x, got_y, got_corner,
     load_sems, send_sems, recv_sems) = scratch

    loads = [
        pltpu.make_async_copy(src, dst, load_sems.at[index])
        for index, (src, dst) in enumerate(
            [(down_in, down), (along_in, along), (cells_in, cells), (masses_in, masses),
             (nodes_in, nodes)]
        )
    ]
    for load in loads:
        load.start()
    loads[0].wait()
    loads[1].wait()

    lanes = lax.broadcasted_iota(jnp.int32, (ROWS, 216), 1)
    to_rows = [one_hot(lanes == down[:, c : c + 1]).astype(BF16) for c in range(2)]
    places = lax.broadcasted_iota(jnp.int32, (216, ROWS), 0)
    to_columns = [one_hot(places == along[c : c + 1, :]).astype(BF16) for c in range(2)]

    loads[2].wait()
    first = dot(to_rows[0], cells[0, 0, 0]).astype(BF16)
    second = dot(to_rows[1], cells[0, 0, 1]).astype(BF16)
    matrix = (dot(first, to_columns[0]) + dot(second, to_columns[1])).astype(BF16)
    rim_matrix[...] = matrix[:, :RIM]
    inner_matrix[...] = matrix[:, RIM:]

    loads[3].wait()
    mass_pad[...] = jnp.zeros(mass_pad.shape, F32)
    for x in range(6):
        high, rest = split(masses[x])
        low, least = split(masses[x] - high.astype(F32))
        mass_pad[8 * x : 8 * x + 6, 0:11] = high.astype(F32)
        mass_pad[8 * x : 8 * x + 6, 16:27] = low.astype(F32)
        mass_pad[8 * x : 8 * x + 6, 32:43] = least.astype(F32)
    pick = one_hot(lax.broadcasted_iota(jnp.int32, (ROWS, 48), 1) == down[:, 2:3]).astype(BF16)
    spread = dot(pick, mass_pad[...].astype(BF16))
    lane = lax.broadcasted_iota(jnp.int32, (ROWS, 128), 1)
    mass = jnp.sum(
        jnp.where(lane % 16 == down[:, 3:4], spread, 0.0), axis=1, keepdims=True
    )
    weight = mass * down[:, 4:5].astype(F32)
    scale1 = 1.0 / (HALF_SPAN * mass)
    shift = CENTER_SHIFT / HALF_SPAN

    loads[4].wait()
    for x in range(6):
        for z in range(11):
            for half in range(2):
                padded[half, 8 * (11 * x + z) : 8 * (11 * x + z) + 6] = nodes[
                    x, z, :, 128 * half : 128 * half + 128
                ].astype(F32)
    for (x, y), start in STARTS.items():
        for half in range(2):
            for low, skip in ((0, 0), (6, 40)):
                states[0, half, start + low : start + low + 6] = padded[
                    half, pl.ds(88 * x + skip + y, 6, stride=8)
                ]
    rim, inner = slice(0, RIM), slice(RIM, ROWS)
    for half in range(2):
        rim_rounded[half] = states[0, half, rim].astype(BF16)
        inner_rounded[half] = states[0, half, inner].astype(BF16)

    buffers = {"x": (sent_x, got_x), "y": (sent_y, got_y), "corner": (sent_corner, got_corner)}

    def moves_of(step, half):
        return [
            remote(
                sizes, buffers[kind][0].at[step, half, here], buffers[kind][1].at[step, half, there],
                send_sems.at[step, half, index], recv_sems.at[step, half, index], (dx, dy),
            )
            for index, (dx, dy, kind, here, there) in enumerate(MESSAGES)
        ]

    def advance(step, half, product, rows):
        if step == 0:
            return product * scale1[rows] - shift * states[0, half, rows]
        return (
            (2.0 * product) * scale1[rows]
            - (2.0 * shift) * states[step, half, rows]
            - states[step - 1, half, rows]
        )

    moves = {}

    def launch(step, half, ahead):
        product = ahead + dot(rim_matrix[rim], rim_rounded[half])
        sums[step, half] = product
        corners = [product[12 * i : 12 * i + 12] for i in range(4)]
        for i in range(4):
            sent_corner[step, half, i] = corners[i]
        sent_x[step, half, 0] = jnp.concatenate([corners[0], corners[2], product[48:96]], axis=0)
        sent_x[step, half, 1] = jnp.concatenate([corners[1], corners[3], product[96:144]], axis=0)
        sent_y[step, half, 0] = jnp.concatenate([product[0:24], product[144:192]], axis=0)
        sent_y[step, half, 1] = jnp.concatenate([product[24:48], product[192:240]], axis=0)
        if step == 0 and half == 0:
            ready()
        moves[step, half] = moves_of(step, half)
        for move in moves[step, half]:
            move.start()

    def inside(step, half):
        inner_next = advance(
            step,
            half,
            dot(rim_matrix[inner], rim_rounded[half])
            + dot(inner_matrix[inner], inner_rounded[half]),
            inner,
        )
        states[step + 1, half, inner] = inner_next
        if step == FILTER_DEG - 1:
            return inner_next
        inner_rounded[half] = inner_next.astype(BF16)
        return dot(inner_matrix[rim], inner_rounded[half])

    def finish(step, half):
        for move in moves[step, half]:
            move.wait_recv()
        own = sums[step, half]
        x0, x5 = got_x[step, half, 0], got_x[step, half, 1]
        y0, y5 = got_y[step, half, 0], got_y[step, half, 1]
        far = [got_corner[step, half, i] for i in range(4)]
        theirs = jnp.concatenate(
            [
                x0[0:12] + y0[0:12] + far[0],
                x5[0:12] + y0[12:24] + far[1],
                x0[12:24] + y5[0:12] + far[2],
                x5[12:24] + y5[12:24] + far[3],
                x0[24:72],
                x5[24:72],
                y0[24:72],
                y5[24:72],
            ],
            axis=0,
        )
        rim_next = advance(step, half, own + theirs, rim)
        states[step + 1, half, rim] = rim_next
        rim_rounded[half] = rim_next.astype(BF16)
        return rim_next

    for half in range(2):
        launch(0, half, dot(inner_matrix[rim], inner_rounded[half]))
    ahead = [inside(0, half) for half in range(2)]
    for step in range(FILTER_DEG - 1):
        for half in range(2):
            finish(step, half)
            launch(step + 1, half, ahead[half])
        for half in range(2):
            ahead[half] = inside(step + 1, half)
    grams = gram(jnp.concatenate(ahead, axis=1), weight[inner])
    keep = lambda a: jnp.concatenate([a[0:24], a[48:96], a[144:192]], axis=0)
    rims = [keep(finish(FILTER_DEG - 1, half)) for half in range(2)]
    rim_grams = gram(jnp.concatenate(rims, axis=1), keep(weight[rim]))
    return tuple(a + b for a, b in zip(grams, rim_grams)), sum(moves.values(), [])


def whole_rows(states):
    return jnp.concatenate([states[FILTER_DEG, 0], states[FILTER_DEG, 1]], axis=1)


def rotate_phase(filtered, factor, padded, out):
    result = dot3(filtered, factor)
    for (x, y), start in STARTS.items():
        for half in range(2):
            lanes = slice(128 * half, 128 * half + 128)
            padded[half, pl.ds(88 * x + y, 6, stride=8)] = result[start : start + 6, lanes]
            padded[half, pl.ds(88 * x + 48 + y, 5, stride=8)] = result[
                start + 7 : start + 12, lanes
            ]
    for x in range(6):
        for z in range(11):
            low = 8 * (11 * x + z)
            out[x, z] = jnp.concatenate(
                [padded[0, low : low + 6], padded[1, low : low + 6]], axis=1
            ).astype(BF16)


def fused_kernel(sizes, node_total, *refs):
    inputs, out, scratch, extra = refs[:5], refs[5], refs[6:28], refs[28:]
    (own, row_in, part, column_in, whole,
     row_send, row_recv, col_send, col_recv, all_send, all_recv) = extra
    n_gx, n_gy = sizes
    my_y = lax.axis_index("gy")
    ready = greet(
        sizes,
        HALO_OFFSETS + [(0, d) for d in range(1, n_gy)] + [(d, 0) for d in range(1, n_gx)],
    )
    grams, moves = filter_phase(sizes, inputs, scratch, ready)
    pieces, height = own.shape[0], own.shape[2] - 1
    packed, diagonal = pack(grams)
    row_moves, col_moves, all_moves = [], [], []
    for p in range(pieces):
        for index in range(n_gy):
            low = (index * pieces + p) * height
            own[p, index, 0:height] = packed[low : low + height]
            own[p, index, height : height + 1] = diagonal
        row_moves.append([
            remote(sizes, own.at[p, lax.rem(my_y + d, n_gy)], row_in.at[p, d - 1],
                   row_send.at[p, d - 1], row_recv.at[p, d - 1], (0, d))
            for d in range(1, n_gy)
        ])
        for move in row_moves[p]:
            move.start()
        col_moves.append([
            remote(sizes, part.at[p], column_in.at[p, d - 1],
                   col_send.at[p, d - 1], col_recv.at[p, d - 1], (d, 0))
            for d in range(1, n_gx)
        ])
        all_moves.append([
            remote(sizes, whole.at[p, my_y], whole.at[p, my_y],
                   all_send.at[p, d - 1], all_recv.at[p, d - 1], (0, d))
            for d in range(1, n_gy)
        ])

    def second(p):
        for move in row_moves[p]:
            move.wait_recv()
        total = own[p, my_y]
        for d in range(1, n_gy):
            total = total + row_in[p, d - 1]
        part[p] = total
        for move in col_moves[p]:
            move.start()

    def third(p):
        for move in col_moves[p]:
            move.wait_recv()
        total = part[p]
        for d in range(1, n_gx):
            total = total + column_in[p, d - 1]
        whole[p, my_y] = total
        for move in all_moves[p]:
            move.start()

    for p in range(pieces):
        second(p)
        if p >= 1:
            third(p - 1)
    third(pieces - 1)
    for p in range(pieces):
        for move in all_moves[p]:
            move.wait_recv()
    packed = jnp.concatenate(
        [whole[p, index, 0:height] for index in range(n_gy) for p in range(pieces)], axis=0
    )
    stacked = unpack(packed, whole[0, 0, height : height + 1])
    factor = inverse_root(stacked, node_total)
    rotate_phase(whole_rows(scratch[9]), factor, scratch[5], out)
    for move in moves + sum(row_moves + col_moves + all_moves, []):
        move.wait_send()


def filter_kernel(sizes, *refs):
    inputs, filtered, stacked, scratch = refs[:5], refs[5], refs[6], refs[7:]
    grams, moves = filter_phase(sizes, inputs, scratch, greet(sizes, HALO_OFFSETS))
    stacked[...] = jnp.concatenate(grams, axis=0)
    filtered[...] = whole_rows(scratch[9])
    for move in moves:
        move.wait_send()


def rotate_kernel(node_total, filtered, stacked, out, padded):
    rotate_phase(filtered[...], inverse_root(stacked[...], node_total), padded, out)


def body(orbitals, masses, cell_matrices):
    n_gx, n_gy = lax.axis_size("gx"), lax.axis_size("gy")
    sizes = (n_gx, n_gy)
    assert orbitals.shape == (6, 6, 11, 256) and cell_matrices.shape == (1, 1, 2, 216, 216)
    node_total = 5 * n_gx * 5 * n_gy * 11
    nodes = jnp.transpose(orbitals, (0, 2, 1, 3))
    down, along = tables()
    arguments = (nodes, masses, cell_matrices, jnp.asarray(down), jnp.asarray(along))
    vmem = pl.BlockSpec(memory_space=pltpu.VMEM)
    hbm = pl.BlockSpec(memory_space=pltpu.MemorySpace.HBM)
    filter_scratch = [
        pltpu.VMEM(nodes.shape, BF16),
        pltpu.VMEM(masses.shape, F32),
        pltpu.VMEM(cell_matrices.shape, BF16),
        pltpu.VMEM(down.shape, jnp.int32),
        pltpu.VMEM(along.shape, jnp.int32),
        pltpu.VMEM((2, 528, 128), F32),
        pltpu.VMEM((48, 128), F32),
        pltpu.VMEM((ROWS, RIM), BF16),
        pltpu.VMEM((ROWS, INNER), BF16),
        pltpu.VMEM((FILTER_DEG + 1, 2, ROWS, 128), F32),
        pltpu.VMEM((2, RIM, 128), BF16),
        pltpu.VMEM((2, INNER, 128), BF16),
        pltpu.VMEM((FILTER_DEG, 2, RIM, 128), F32),
    ]
    filter_scratch += [
        pltpu.VMEM((FILTER_DEG, 2) + shape + (128,), F32)
        for shape in ((2, 72), (2, 72), (4, 12)) * 2
    ]
    filter_scratch += [
        pltpu.SemaphoreType.DMA((5,)),
        pltpu.SemaphoreType.DMA((FILTER_DEG, 2, len(MESSAGES))),
        pltpu.SemaphoreType.DMA((FILTER_DEG, 2, len(MESSAGES))),
    ]
    params = pltpu.CompilerParams(
        collective_id=0, has_side_effects=True, vmem_limit_bytes=VMEM_BYTES
    )
    if 256 % (8 * PIECES * n_gy) == 0:
        height = 256 // n_gy // PIECES + 1
        result = pl.pallas_call(
            functools.partial(fused_kernel, sizes, node_total),
            out_shape=jax.ShapeDtypeStruct(nodes.shape, BF16),
            in_specs=[hbm] * 5,
            out_specs=vmem,
            scratch_shapes=filter_scratch
            + [
                pltpu.VMEM((PIECES, n_gy, height, 128), F32),
                pltpu.VMEM((PIECES, n_gy - 1, height, 128), F32),
                pltpu.VMEM((PIECES, height, 128), F32),
                pltpu.VMEM((PIECES, n_gx - 1, height, 128), F32),
                pltpu.VMEM((PIECES, n_gy, height, 128), F32),
            ]
            + [pltpu.SemaphoreType.DMA((PIECES, n - 1)) for n in (n_gy, n_gy, n_gx, n_gx, n_gy, n_gy)],
            compiler_params=params,
        )(*arguments)
    else:
        filtered, stacked = pl.pallas_call(
            functools.partial(filter_kernel, sizes),
            out_shape=[
                jax.ShapeDtypeStruct((ROWS, 256), F32),
                jax.ShapeDtypeStruct((384, 128), F32),
            ],
            in_specs=[hbm] * 5,
            out_specs=[vmem] * 2,
            scratch_shapes=filter_scratch,
            compiler_params=params,
        )(*arguments)
        stacked = lax.psum(stacked, ("gx", "gy"))
        result = pl.pallas_call(
            functools.partial(rotate_kernel, node_total),
            out_shape=jax.ShapeDtypeStruct(nodes.shape, BF16),
            in_specs=[vmem] * 2,
            out_specs=vmem,
            scratch_shapes=[pltpu.VMEM((2, 528, 128), F32)],
            compiler_params=pltpu.CompilerParams(vmem_limit_bytes=VMEM_BYTES),
        )(filtered, stacked)
    return jnp.transpose(result, (0, 2, 1, 3))


def solution(mesh):
    return jax.shard_map(
        body,
        mesh=mesh,
        in_specs=(P("gx", "gy", None, None), P("gx", "gy", None), P("gx", "gy", None, None, None)),
        out_specs=P("gx", "gy", None, None),
        check_vma=False,
    )
```
